32 devices in a mesh: dp: 8 (over y, x, core), tensor: 4 (over z).
Axes of the slice: x: 2, y: 2, z: 4, core: 2. Of those that a mesh axis runs over, the one named last changes fastest.
Arguments:
- frames: bfloat16 [2, 8, 1152, 1024], P(None, 'dp'), may hold values from -6 to 6
- skip_frames: bfloat16 [2, 8, 1152, 1024], P(None, 'dp'), may hold values from -6 to 6
- cotangent: bfloat16 [2, 8, 1152, 1024], P(None, 'dp'), may hold values from -6 to 6
- lengths: int32 [2, 8], P(None, 'dp'), may hold values from 288 to 1152, as said below
- time_steps: int32 [2, 8], P(None, 'dp'), may hold values from 0 to 63
- time_table: bfloat16 [64, 1024], replicated, may hold values from -6 to 6
- w_skip: bfloat16 [2048, 1024], replicated, may hold values from -0.125 to 0.125
- w_gamma_attn: bfloat16 [1024, 1024], replicated, may hold values from -0.1875 to 0.1875
- w_gamma_ffn: bfloat16 [1024, 1024], replicated, may hold values from -0.1875 to 0.1875
- w_qkv: bfloat16 [3, 1024, 1024], P(None, None, 'tensor'), may hold values from -0.1875 to 0.1875
- w_out: bfloat16 [1024, 1024], P('tensor'), may hold values from -0.75 to 0.75
- w_up: bfloat16 [1024, 4096], P(None, 'tensor'), may hold values from -0.1875 to 0.1875
- b_up: bfloat16 [4096], P('tensor'), may hold values from -4 to 4
- w_down: bfloat16 [4096, 1024], P('tensor'), may hold values from -0.09375 to 0.09375
Outputs:
- mixed: bfloat16 [2, 8, 1152, 1024], P(None, 'dp')
- grad_frames: bfloat16 [2, 8, 1152, 1024], P(None, 'dp')
- grad_skip: bfloat16 [2, 8, 1152, 1024], P(None, 'dp')
- grad_table: float32 [64, 1024], P('dp')
- grad_w_skip: float32 [2048, 1024], P(('dp', 'tensor'))
- grad_w_gamma_attn: float32 [1024, 1024], P('dp')
- grad_w_gamma_ffn: float32 [1024, 1024], P('dp')
- grad_w_qkv: float32 [3, 1024, 1024], P(None, 'dp', 'tensor')
- grad_w_out: float32 [1024, 1024], P('tensor', 'dp')
- grad_w_up: float32 [1024, 4096], P('dp', 'tensor')
- grad_b_up: float32 [4096], P('tensor')
- grad_w_down: float32 [4096, 1024], P('tensor', 'dp')
The draws below stay inside these ranges and needn't reach their ends.
Inputs may be any that keep to these rules, and one draw needn't show every extreme that they name: `lengths`: the live frames of an utterance are its first slots; in every micro-batch one utterance fills all 1152 slots.
All inputs are finite; a program needn't handle non-finite values.
Results may differ from the reference program's by a relative error of at most 0.025.
The reference program's roundings to bfloat16 on the way count: a program that leaves them out, or rounds other values in their place, can miss the bound.
Values may be sent and summed in bfloat16 or wider, within the bound.
No kernel may reach another device: no remote copies, remote signals or barrier semaphores. Data moves between devices by JAX's collectives and lax.ppermute only.
A program may use at most 256 MiB of HBM per device.

```python
import math
import jax
import jax.numpy as jnp
from jax import lax

D = 1024
HEADS = 16
HD = 64
FF = 4096
L = 1152
MB = 2
NT = 64
BATCH = 8
N_TENSOR = 4


def draw_lengths(key, part):
    key_base, key_full = jax.random.split(key)
    spread_draw = jax.random.randint(key_base, (MB, BATCH), 0, L)
    base_length = L // 4 + spread_draw * spread_draw // L * 3 // 4
    full_slot = jax.random.randint(key_full, (MB, 1), 0, BATCH)
    slots = jnp.arange(BATCH)[None, :]
    return jnp.where(slots == full_slot, L, base_length).astype(jnp.int32)


def touch_ends(result, own_key, least, largest):
    place = [jax.random.randint(jax.random.fold_in(own_key, axis), (), 0, length) for axis, length in enumerate(result.shape)]
    main_axis = result.shape.index(max(result.shape))
    neighbour = place[:main_axis] + [(place[main_axis] + 1) % result.shape[main_axis]] + place[main_axis + 1:]
    return result.at[tuple(place)].set(least).at[tuple(neighbour)].set(largest)


def steps_of(rng, shape, cuts, smallest, largest):
    gain = 1.0
    for axis_at, blocks in cuts:
        draws = jax.random.uniform(jax.random.fold_in(jax.random.fold_in(rng, 6), axis_at), (blocks,), jnp.float32, smallest / len(cuts), largest / len(cuts))
        gain = gain * jnp.repeat(jnp.exp(draws), shape[axis_at] // blocks).reshape((-1,) + (1,) * (len(shape) - 1 - axis_at))
    return gain


def gaussian(own_key, shape, deviation, most, pieces=(), kind=jnp.bfloat16):
    drawn = deviation * jax.random.normal(own_key, shape, jnp.float32)
    if pieces:
        drawn = drawn * steps_of(own_key, shape, pieces, -0.22, 0.18)
    return jnp.clip(drawn, -most, most).astype(kind)


def setup_inputs(seed: int = 0) -> dict:
    seeds = jax.random.split(jax.random.key(seed), 15)
    return {
        "frames": gaussian(seeds[0], (MB, BATCH, L, D), 1.0, 6.0, ((1, 8),)),
        "skip_frames": gaussian(seeds[1], (MB, BATCH, L, D), 1.0, 6.0, ((1, 8),)),
        "cotangent": gaussian(seeds[2], (MB, BATCH, L, D), 1.0, 6.0, ((1, 8),)),
        "lengths": draw_lengths(jax.random.fold_in(seeds[14], 71), 0),
        "time_steps": touch_ends(jax.random.randint(seeds[4], (MB, BATCH), 0, NT), jax.random.fold_in(seeds[4], 1), 0, NT - 1).astype(jnp.int32),
        "time_table": gaussian(seeds[5], (NT, D), 1.0, 6.0),
        "w_skip": gaussian(seeds[6], (2 * D, D), (2 * D) ** -0.5, 0.125),
        "w_gamma_attn": gaussian(seeds[7], (D, D), D ** -0.5, 0.1875),
        "w_gamma_ffn": gaussian(seeds[8], (D, D), D ** -0.5, 0.1875),
        "w_qkv": gaussian(seeds[9], (3, D, D), D ** -0.5, 0.1875, ((2, 4),)),
        "w_out": gaussian(seeds[10], (D, D), HD ** -0.5, 0.75, ((0, 4),)),
        "w_up": gaussian(seeds[11], (D, FF), D ** -0.5, 0.1875, ((1, 4),)),
        "b_up": gaussian(seeds[12], (FF,), 1.0, 4.0, ((0, 4),)),
        "w_down": gaussian(seeds[13], (FF, D), FF ** -0.5, 0.09375, ((0, 4),)),
    }


EPSILON = 1e-06
MASKED = -1e+30
PRECISE = lax.Precision.HIGHEST

@jax.custom_vjp
def low(v):
    return lax.optimization_barrier(v.astype(jnp.bfloat16)).astype(jnp.float32)

@jax.custom_vjp
def low_back(v):
    return v

def low_keep(v):
    return (low(v), None)

def low_pass(kept, grad):
    return (grad,)

def back_keep(v):
    return (v, None)

def back_low(kept, grad):
    return (low(grad),)
low.defvjp(low_keep, low_pass)
low_back.defvjp(back_keep, back_low)

def rope_tables(length, head_size):
    half_size = head_size // 2
    places = jnp.arange(length, dtype=jnp.float32)
    frequency = jnp.exp(jnp.arange(half_size, dtype=jnp.float32) * (-2.0 * math.log(10000.0) / head_size))
    angles = places[:, None] * frequency[None, :]
    return (jnp.cos(angles)[:, None, :], jnp.sin(angles)[:, None, :])

def rotate(values, cosine, sine):
    half_size = values.shape[-1] // 2
    front_half = values[..., :half_size]
    back_half = values[..., half_size:]
    return jnp.concatenate([front_half * cosine - back_half * sine, back_half * cosine + front_half * sine], axis=-1)

def normalize(hidden):
    return hidden * lax.rsqrt(lax.optimization_barrier(jnp.mean(hidden * hidden, axis=-1, keepdims=True)) + EPSILON)

def utterance(params, frame_rows, skip_rows, length_value, step_value):
    time_table, w_skip, w_gamma_attn, w_gamma_ffn, w_qkv, w_out, w_up, b_up, w_down = params
    groups = N_TENSOR
    local_width = D // groups
    ff_local = FF // groups
    heads_local = HEADS // groups
    places = jnp.arange(L)
    live_keys = places < length_value
    condition = lax.dynamic_index_in_dim(time_table, step_value, 0, keepdims=False)
    gain_attn = 1.0 + low_back(jnp.dot(condition, w_gamma_attn, precision=PRECISE))
    gain_ffn = 1.0 + low_back(jnp.dot(condition, w_gamma_ffn, precision=PRECISE))
    joined = jnp.concatenate([frame_rows, skip_rows], axis=-1)
    skip_mixed = low_back(jnp.dot(joined, w_skip, precision=PRECISE))
    attn_in = normalize(skip_mixed) * gain_attn[None, :]
    spread_in = low_back(jnp.broadcast_to(low(attn_in)[None], (groups, L, D)))
    projected = low_back(jnp.einsum('gld,cdge->cgle', spread_in, w_qkv.reshape(3, D, groups, local_width), precision=PRECISE))
    projected = projected.reshape(3, groups, L, heads_local, HD).transpose(0, 2, 1, 3, 4).reshape(3, L, HEADS, HD)
    cosine, sine = rope_tables(L, HD)
    queries = low(rotate(projected[0], cosine, sine))
    keys_rot = low(rotate(projected[1], cosine, sine))
    values = low(projected[2])
    raw_scores = low_back(jnp.einsum('lhe,mhe->hlm', queries, keys_rot, precision=PRECISE) * (1.0 / math.sqrt(HD)))
    raw_scores = jnp.where(live_keys[None, None, :], raw_scores, MASKED)
    maxima = lax.optimization_barrier(jnp.max(raw_scores, axis=-1, keepdims=True))
    exponent = jnp.exp(raw_scores - maxima)
    probs = exponent / lax.optimization_barrier(jnp.sum(exponent, axis=-1, keepdims=True))
    context = low(low_back(jnp.einsum('hlm,mhe->lhe', low(probs), values, precision=PRECISE)))
    context = context.reshape(L, groups, local_width)
    attn_parts = jnp.einsum('lge,ged->gld', context, w_out.reshape(groups, local_width, D), precision=PRECISE)
    attn_total = low_back(lax.optimization_barrier(jnp.sum(low(attn_parts), axis=0)))
    middle = skip_mixed + attn_total
    ffn_in = normalize(middle) * gain_ffn[None, :]
    spread_ffn = low_back(jnp.broadcast_to(low(ffn_in)[None], (groups, L, D)))
    pre_act = low_back(jnp.einsum('gld,dgf->glf', spread_ffn, w_up.reshape(D, groups, ff_local), precision=PRECISE) + b_up.reshape(groups, 1, ff_local))
    activated = low(jax.nn.gelu(pre_act, approximate=False))
    ffn_parts = jnp.einsum('glf,gfd->gld', activated, w_down.reshape(groups, ff_local, D), precision=PRECISE)
    ffn_total = lax.optimization_barrier(jnp.sum(low(ffn_parts), axis=0))
    return (middle + ffn_total) * live_keys[:, None].astype(jnp.float32)

def reference(frames, skip_frames, cotangent, lengths, time_steps, time_table, w_skip, w_gamma_attn, w_gamma_ffn, w_qkv, w_out, w_up, b_up, w_down):
    utter_count = MB * BATCH
    floats = tuple((weight.astype(jnp.float32) for weight in (time_table, w_skip, w_gamma_attn, w_gamma_ffn, w_qkv, w_out, w_up, b_up, w_down)))
    frame_flat = frames.astype(jnp.float32).reshape(utter_count, L, D)
    skip_flat = skip_frames.astype(jnp.float32).reshape(utter_count, L, D)
    length_flat = lengths.reshape(utter_count).astype(jnp.int32)
    step_flat = time_steps.reshape(utter_count).astype(jnp.int32)

    def forward(frame_all, skip_all, params):
        checked = jax.checkpoint(utterance)

        def scan_item(carry, packed):
            return (carry, checked(params, packed[0], packed[1], packed[2], packed[3]))
        _, outputs = lax.scan(scan_item, jnp.zeros((), jnp.float32), (frame_all, skip_all, length_flat, step_flat))
        return outputs
    outputs, backward = jax.vjp(forward, frame_flat, skip_flat, floats)
    grad_frames, grad_skip, grads = backward(cotangent.astype(jnp.float32).reshape(utter_count, L, D))
    shape_full = (MB, BATCH, L, D)
    return (outputs.reshape(shape_full).astype(jnp.bfloat16), grad_frames.reshape(shape_full).astype(jnp.bfloat16), grad_skip.reshape(shape_full).astype(jnp.bfloat16), grads[0], grads[1], grads[2], grads[3], grads[4], grads[5], grads[6], grads[7], grads[8])
```

```python
import functools
import math

import jax
import jax.numpy as jnp
from jax import lax
from jax.experimental import pallas as pl
from jax.experimental.pallas import tpu as pltpu
from jax.sharding import PartitionSpec as P

HD = 64
LANES = 128
EPSILON = 1e-06
MASKED = -1e30
BF16 = jnp.bfloat16
F32 = jnp.float32
SCALE = 1.0 / math.sqrt(HD)
VMEM_BYTES = 62 * 1024 * 1024
BOTH = ("dp", "tensor")


def dot(a, b):
    return lax.dot_general(a, b, (((1,), (0,)), ((), ())), preferred_element_type=F32)


def dot_t(a, b):
    return lax.dot_general(a, b, (((1,), (1,)), ((), ())), preferred_element_type=F32)


def t_dot(a, b):
    return lax.dot_general(a, b, (((0,), (0,)), ((), ())), preferred_element_type=F32)


def rope_tables(length):
    lane = jnp.arange(LANES)
    half = HD // 2
    frequency = jnp.exp((lane % half).astype(F32) * (-2.0 * math.log(10000.0) / HD))
    angles = jnp.arange(length, dtype=F32)[:, None] * frequency[None, :]
    sign = jnp.where(lane % HD < half, -1.0, 1.0)
    return jnp.cos(angles), jnp.sin(angles) * sign[None, :]


def partner(x):
    lane = lax.broadcasted_iota(jnp.int32, x.shape, 1)
    return jnp.where(lane & (HD - 1) < HD // 2, pltpu.roll(x, LANES - HD // 2, 1), pltpu.roll(x, HD // 2, 1))


def head_masks(dtype):
    lane = lax.broadcasted_iota(jnp.int32, (1, LANES), 1)
    return (lane < HD).astype(dtype), (lane >= HD).astype(dtype)


def call(kernel, grid, in_specs, out_specs, out_shape, scratch=(), prefetch=1, flops=0, nbytes=0):
    return pl.pallas_call(
        kernel,
        out_shape=out_shape,
        grid_spec=pltpu.PrefetchScalarGridSpec(
            num_scalar_prefetch=prefetch,
            grid=grid,
            in_specs=in_specs,
            out_specs=out_specs,
            scratch_shapes=list(scratch),
        ),
        compiler_params=pltpu.CompilerParams(
            dimension_semantics=("arbitrary",) * len(grid), vmem_limit_bytes=VMEM_BYTES
        ),
        cost_estimate=pl.CostEstimate(flops=flops, bytes_accessed=nbytes, transcendentals=0),
    )


def whole(shape):
    return pl.BlockSpec(shape, lambda *_: (0,) * len(shape), pipeline_mode=pl.Buffered(1))


def row_block(length, wanted):
    for rows in (wanted, 384, 288, 192, 128, 64, 32, 16):
        if rows <= wanted and length % rows == 0:
            return rows
    return length


def base_kernel(len_ref, f_ref, s_ref, w_ref, g_ref, base_ref, ain_ref, *, rows, width):
    live = pl.program_id(1) * rows < len_ref[pl.program_id(0)]

    @pl.when(live)
    def _():
        acc = dot(f_ref[0], w_ref[:width]) + dot(s_ref[0], w_ref[width:])
        factor = lax.rsqrt(jnp.mean(acc * acc, axis=-1, keepdims=True) + EPSILON)
        base_ref[0] = acc
        ain_ref[0] = (acc * factor * g_ref[0]).astype(BF16)

    @pl.when(jnp.logical_not(live))
    def _():
        base_ref[...] = jnp.zeros_like(base_ref)
        ain_ref[...] = jnp.zeros_like(ain_ref)


def base_call(lengths, frames, skip, w_skip, gain):
    units, length, width = frames.shape
    rows = row_block(length, 384)
    block = pl.BlockSpec((1, rows, width), lambda u, i, *_: (u, i, 0))
    return call(
        functools.partial(base_kernel, rows=rows, width=width),
        (units, length // rows),
        [block, block, whole(w_skip.shape), pl.BlockSpec((1, 1, width), lambda u, i, *_: (u, 0, 0))],
        [block, block],
        [
            jax.ShapeDtypeStruct(frames.shape, F32),
            jax.ShapeDtypeStruct(frames.shape, BF16),
        ],
        flops=4 * units * length * width * width,
        nbytes=units * length * width * 10,
    )(lengths, frames, skip, w_skip, gain)


def qkv_kernel(len_ref, a_ref, w_ref, cos_ref, sin_ref, o_ref, *, rows, groups, width, group_width):
    live = pl.program_id(1) * rows < len_ref[pl.program_id(0)]

    @pl.when(live)
    def _():
        a = a_ref[0]
        cosine = cos_ref[...]
        sine = sin_ref[...]
        for g in range(groups):
            for c in range(3):
                y = dot(a, w_ref[:, g, c].reshape(width, group_width))
                for j in range(group_width // LANES):
                    part = y[:, j * LANES : (j + 1) * LANES]
                    if c < 2:
                        part = part * cosine + partner(part) * sine
                    if c == 0:
                        part = part * SCALE
                    at = g * group_width + j * LANES
                    o_ref[c, 0, :, at : at + LANES] = part.astype(BF16)

    @pl.when(jnp.logical_not(live))
    def _():
        o_ref[...] = jnp.zeros_like(o_ref)


def qkv_call(lengths, attn_in, wqkv, cosine, sine):
    units, length, width = attn_in.shape
    groups, group_width = wqkv.shape[1], wqkv.shape[4]
    total = groups * group_width
    rows = row_block(length, 384)
    table = pl.BlockSpec((rows, LANES), lambda u, i, *_: (i, 0))
    return call(
        functools.partial(qkv_kernel, rows=rows, groups=groups, width=width, group_width=group_width),
        (units, length // rows),
        [pl.BlockSpec((1, rows, width), lambda u, i, *_: (u, i, 0)), whole(wqkv.shape), table, table],
        pl.BlockSpec((3, 1, rows, total), lambda u, i, *_: (0, u, i, 0)),
        jax.ShapeDtypeStruct((3, units, length, total), BF16),
        flops=6 * units * length * width * total,
        nbytes=units * length * width * 8,
    )(lengths, attn_in, wqkv, cosine, sine)


def extents_of(length):
    step = length // 3
    return [e for e in (step, step + step * 2 // 3, 2 * step + step // 3, length) if e % 128 == 0]


def by_extent(n, extents, run):
    low = 0
    for e in extents:
        pl.when(jnp.logical_and(n > low, n <= e))(functools.partial(run, e, low))
        low = e


def attn_kernel(len_ref, q_ref, k_ref, v_ref, ctx_ref, st_ref, *, length, block, extents):
    u = pl.program_id(0)
    p = pl.program_id(1)
    n = len_ref[u]
    lane = lax.broadcasted_iota(jnp.int32, (block, LANES), 1)
    masks = head_masks(BF16)

    @pl.when(p == 0)
    def _():
        st_ref[...] = jnp.zeros_like(st_ref)

    def run(extent, low):
        keys = k_ref[0, 0, :extent]
        values = v_ref[0, 0, :extent]
        place = lax.broadcasted_iota(jnp.int32, (1, extent), 1)
        bias = jnp.where(place < n, 0.0, MASKED)

        def body(i, carry):
            at = pl.ds(pl.multiple_of(i * block, block), block)
            q = q_ref[0, 0, at]
            stats = st_ref[0, at]
            outs = []
            for h in range(2):
                s = dot_t(q * masks[h], keys) + bias
                m = jnp.max(s, axis=-1, keepdims=True)
                e = jnp.exp(s - m)
                l = jnp.sum(e, axis=-1, keepdims=True)
                outs.append(dot(e.astype(BF16), values) * (1.0 / l))
                stats = jnp.where(lane == 2 * p + h, m + jnp.log(l), stats)
            ctx_ref[0, at] = jnp.where(lane < HD, outs[0], outs[1]).astype(BF16)
            st_ref[0, at] = stats
            return carry

        lax.fori_loop(0, pl.cdiv(n, block), body, 0)

    by_extent(n, extents, run)

    def clear(i, carry):
        at = pl.ds(pl.multiple_of(i * block, block), block)
        ctx_ref[0, at] = jnp.zeros((block, LANES), BF16)
        return carry

    lax.fori_loop(pl.cdiv(n, block), length // block, clear, 0)


def attn_call(lengths, qkv):
    _, units, length, total = qkv.shape
    block = row_block(length, 128)
    pairs = total // LANES

    def part(c):
        return pl.BlockSpec((1, 1, length, LANES), lambda u, p, *_: (c, u, 0, p))

    return call(
        functools.partial(attn_kernel, length=length, block=block, extents=extents_of(length)),
        (units, pairs),
        [part(0), part(1), part(2)],
        [
            pl.BlockSpec((1, length, LANES), lambda u, p, *_: (u, 0, p)),
            pl.BlockSpec((1, length, LANES), lambda u, p, *_: (u, 0, 0)),
        ],
        [
            jax.ShapeDtypeStruct((units, length, total), BF16),
            jax.ShapeDtypeStruct((units, length, LANES), F32),
        ],
        flops=16 * units * length * length * total,
        nbytes=units * length * total * 8,
    )(lengths, qkv, qkv, qkv)


def mid_kernel(
    len_ref,
    own_ref,
    ctx_ref,
    base_ref,
    cot_ref,
    gain_ref,
    wout_ref,
    wup_ref,
    wdown_ref,
    b_ref,
    mixed_ref,
    fin_ref,
    act_ref,
    gpre_ref,
    gmid_ref,
    gattn_ref,
    gctx_ref,
    ggain_ref,
    gbias_ref,
    out_acc,
    gin_acc,
    fin_s,
    cot_s,
    *,
    rows,
    width,
    groups,
    group_width,
    hidden,
    chunk,
):
    u = pl.program_id(0)
    i = pl.program_id(1)
    n = len_ref[u]
    own = own_ref[0]
    live = i * rows < n

    @pl.when(i == 0)
    def _():
        ggain_ref[...] = jnp.zeros_like(ggain_ref)
        gbias_ref[...] = jnp.zeros_like(gbias_ref)

    @pl.when(live)
    def _():
        place = i * rows + lax.broadcasted_iota(jnp.int32, (rows, 1), 0)
        row_live = (place < n).astype(F32)
        attn = jnp.zeros((rows, width), F32)
        for g in range(groups):
            w = wout_ref[:, g].reshape(group_width, width)
            share = dot(ctx_ref[0, :, g * group_width : (g + 1) * group_width], w)
            attn = attn + share.astype(BF16).astype(F32)
        middle = base_ref[0] + attn
        factor = lax.rsqrt(jnp.mean(middle * middle, axis=-1, keepdims=True) + EPSILON)
        gain = gain_ref[0]
        gmid_ref[0] = middle
        fin_s[...] = (middle * factor * gain).astype(BF16)
        fin_ref[0] = fin_s[...]
        cot_s[...] = (cot_ref[0].astype(F32) * row_live).astype(BF16)
        out_acc[...] = jnp.zeros_like(out_acc)
        gin_acc[...] = jnp.zeros_like(gin_acc)

        def step(g, carry):
            share = jnp.zeros((rows, width), F32)
            back = jnp.zeros((rows, width), F32)
            for c in range(hidden // chunk):
                cols = slice(c * chunk, (c + 1) * chunk)
                up = wup_ref[:, g, :, cols].reshape(width, chunk)
                down = wdown_ref[:, g].reshape(hidden, width)[cols]
                pre = dot(fin_s[...], up) + b_ref[g][:, cols].astype(F32)
                grad_act = dot_t(cot_s[...], down)
                phi = 0.5 + 0.5 * lax.erf(pre * math.sqrt(0.5))
                density = jnp.exp(-0.5 * pre * pre) * (1.0 / math.sqrt(2.0 * math.pi))
                act = (pre * phi).astype(BF16)
                grad_pre_wide = (phi + pre * density) * grad_act
                grad_pre = grad_pre_wide.astype(BF16)
                share = share + dot(act, down)
                back = back + dot_t(grad_pre, up)

                @pl.when(g == own)
                def _():
                    act_ref[0, :, cols] = (act.astype(F32) * row_live).astype(BF16)
                    gpre_ref[0, :, cols] = grad_pre
                    gbias_ref[0, :, cols] += jnp.sum(grad_pre.astype(F32), axis=0, keepdims=True)

            out_acc[...] += share.astype(BF16).astype(F32)
            gin_acc[...] += back.astype(BF16).astype(F32)
            return carry

        lax.fori_loop(0, wup_ref.shape[1], step, 0)
        middle = gmid_ref[0]
        factor = lax.rsqrt(jnp.mean(middle * middle, axis=-1, keepdims=True) + EPSILON)
        normed = middle * factor
        mixed_ref[0] = ((middle + out_acc[...]) * row_live).astype(BF16)
        grad_in = gin_acc[...]
        ggain_ref[0] += jnp.sum(grad_in * normed, axis=0, keepdims=True)
        dn = grad_in * gain
        grad_middle = cot_s[...].astype(F32) + factor * (
            dn - normed * jnp.mean(dn * normed, axis=-1, keepdims=True)
        )
        gmid_ref[0] = grad_middle
        grad_attn = grad_middle.astype(BF16)
        gattn_ref[0] = grad_attn
        for g in range(groups):
            w = wout_ref[:, g].reshape(group_width, width)
            gctx_ref[0, :, g * group_width : (g + 1) * group_width] = dot_t(grad_attn, w).astype(BF16)

    @pl.when(jnp.logical_not(live))
    def _():
        for ref in (mixed_ref, fin_ref, act_ref, gpre_ref, gmid_ref, gattn_ref, gctx_ref):
            ref[...] = jnp.zeros_like(ref)


def mid_call(lengths, own, context, base, cotangent, gain, wout, wup, wdown, bias):
    units, length, width = base.shape
    groups = wout.shape[1]
    total = context.shape[2]
    hidden = wup.shape[3]
    rows = row_block(length, 384)
    chunk = min(hidden, 512)

    def block(size):
        return pl.BlockSpec((1, rows, size), lambda u, i, *_: (u, i, 0))

    def unit(size):
        return pl.BlockSpec((1, 1, size), lambda u, i, *_: (u, 0, 0))

    def full(size, dtype):
        return jax.ShapeDtypeStruct((units, length, size), dtype)

    ff = wup.shape[1] * hidden
    return call(
        functools.partial(
            mid_kernel,
            rows=rows,
            width=width,
            groups=groups,
            group_width=total // groups,
            hidden=hidden,
            chunk=chunk,
        ),
        (units, length // rows),
        [
            block(total),
            block(width),
            block(width),
            unit(width),
            whole(wout.shape),
            whole(wup.shape),
            whole(wdown.shape),
            whole(bias.shape),
        ],
        [
            block(width),
            block(width),
            block(hidden),
            block(hidden),
            block(width),
            block(width),
            block(total),
            unit(width),
            unit(hidden),
        ],
        [
            full(width, BF16),
            full(width, BF16),
            full(hidden, BF16),
            full(hidden, BF16),
            full(width, F32),
            full(width, BF16),
            full(total, BF16),
            jax.ShapeDtypeStruct((units, 1, width), F32),
            jax.ShapeDtypeStruct((units, 1, hidden), F32),
        ],
        scratch=[
            pltpu.VMEM((rows, width), F32),
            pltpu.VMEM((rows, width), F32),
            pltpu.VMEM((rows, width), BF16),
            pltpu.VMEM((rows, width), BF16),
        ],
        prefetch=2,
        flops=units * length * width * (8 * ff + 4 * total),
        nbytes=units * length * width * 26,
    )(lengths, own, context, base, cotangent, gain, wout, wup, wdown, bias)


def attn_back_kernel(
    len_ref,
    q_ref,
    k_ref,
    v_ref,
    ctx_ref,
    gctx_ref,
    st_ref,
    cos_ref,
    sin_ref,
    o_ref,
    dq_s,
    stat_s,
    delta_s,
    *,
    length,
    block,
    extents,
):
    u = pl.program_id(0)
    p = pl.program_id(1)
    n = len_ref[u]
    masks = head_masks(BF16)

    @pl.when(p == 0)
    def _():
        stat_s[...] = st_ref[0].T

    product = ctx_ref[0].astype(F32) * gctx_ref[0].astype(F32)
    turned = product.T
    delta_s[0:1] = jnp.sum(turned[:HD], axis=0, keepdims=True)
    delta_s[1:2] = jnp.sum(turned[HD:], axis=0, keepdims=True)

    def unturn(x, at):
        return x * cos_ref[at] - partner(x) * sin_ref[at]

    def run(extent, low):
        q = q_ref[0, 0, :extent]
        gctx = gctx_ref[0, :extent]
        dq_s[:extent] = jnp.zeros((extent, LANES), F32)
        lse = [stat_s[pl.ds(2 * p + h, 1), :extent] for h in range(2)]
        delta = [delta_s[h : h + 1, :extent] for h in range(2)]
        lane = lax.broadcasted_iota(jnp.int32, (block, LANES), 1)

        def body(i, carry):
            at = pl.ds(pl.multiple_of(i * block, block), block)
            keys = k_ref[0, 0, at]
            values = v_ref[0, 0, at]
            key_live = (i * block + lax.broadcasted_iota(jnp.int32, (block, 1), 0) < n)
            bias = jnp.where(key_live, 0.0, MASKED)
            grad_v, grad_k, grad_s, masked = [], [], [], []
            for h in range(2):
                kh = keys * masks[h]
                s = dot_t(kh, q)
                probs = jnp.exp(s + bias - lse[h])
                grad_v.append(dot(probs.astype(BF16), gctx))
                gp = dot_t(values * masks[h], gctx)
                gs = (probs * (gp - delta[h])).astype(BF16)
                grad_k.append(dot(gs, q))
                grad_s.append(gs)
                masked.append(kh)
            dq_s[:extent] += t_dot(jnp.concatenate(grad_s, axis=0), jnp.concatenate(masked, axis=0))
            gk = jnp.where(lane < HD, grad_k[0], grad_k[1])
            gv = jnp.where(lane < HD, grad_v[0], grad_v[1])
            o_ref[1, 0, at] = unturn(gk, at).astype(BF16)
            o_ref[2, 0, at] = gv.astype(BF16)
            return carry

        lax.fori_loop(0, pl.cdiv(n, block), body, 0)

    by_extent(n, extents, run)

    def finish(i, carry):
        at = pl.ds(pl.multiple_of(i * block, block), block)
        o_ref[0, 0, at] = (unturn(dq_s[at], at) * SCALE).astype(BF16)
        return carry

    def clear(i, carry):
        at = pl.ds(pl.multiple_of(i * block, block), block)
        for c in range(3):
            o_ref[c, 0, at] = jnp.zeros((block, LANES), BF16)
        return carry

    lax.fori_loop(0, pl.cdiv(n, block), finish, 0)
    lax.fori_loop(pl.cdiv(n, block), length // block, clear, 0)


def attn_back_call(lengths, qkv, context, grad_context, stats, cosine, sine):
    _, units, length, total = qkv.shape
    block = row_block(length, 128)
    pairs = total // LANES

    def part(c):
        return pl.BlockSpec((1, 1, length, LANES), lambda u, p, *_: (c, u, 0, p))

    lanes = pl.BlockSpec((1, length, LANES), lambda u, p, *_: (u, 0, p))
    return call(
        functools.partial(attn_back_kernel, length=length, block=block, extents=extents_of(length)),
        (units, pairs),
        [
            part(0),
            part(1),
            part(2),
            lanes,
            lanes,
            pl.BlockSpec((1, length, LANES), lambda u, p, *_: (u, 0, 0)),
            whole((length, LANES)),
            whole((length, LANES)),
        ],
        pl.BlockSpec((3, 1, length, LANES), lambda u, p, *_: (0, u, 0, p)),
        jax.ShapeDtypeStruct((3, units, length, total), BF16),
        scratch=[
            pltpu.VMEM((length, LANES), F32),
            pltpu.VMEM((LANES, length), F32),
            pltpu.VMEM((8, length), F32),
        ],
        flops=40 * units * length * length * total,
        nbytes=units * length * total * 16,
    )(lengths, qkv, qkv, qkv, context, grad_context, stats, cosine, sine)


def back_kernel(
    len_ref,
    gp_ref,
    w_ref,
    base_ref,
    gmid_ref,
    gain_ref,
    wskip_ref,
    gbase_ref,
    gf_ref,
    gs_ref,
    ggain_ref,
    *,
    rows,
    width,
    groups,
    group_width,
):
    u = pl.program_id(0)
    i = pl.program_id(1)
    live = i * rows < len_ref[u]

    @pl.when(i == 0)
    def _():
        ggain_ref[...] = jnp.zeros_like(ggain_ref)

    @pl.when(live)
    def _():
        grad_in = jnp.zeros((rows, width), F32)
        for g in range(groups):
            cols = slice(g * group_width, (g + 1) * group_width)
            share = jnp.zeros((rows, width), F32)
            for c in range(3):
                share = share + dot_t(gp_ref[c, 0, :, cols], w_ref[:, g, c].reshape(width, group_width))
            grad_in = grad_in + share.astype(BF16).astype(F32)
        base = base_ref[0]
        factor = lax.rsqrt(jnp.mean(base * base, axis=-1, keepdims=True) + EPSILON)
        normed = base * factor
        ggain_ref[0] += jnp.sum(grad_in * normed, axis=0, keepdims=True)
        dm = grad_in * gain_ref[0]
        grad_base = (
            gmid_ref[0] + factor * (dm - normed * jnp.mean(dm * normed, axis=-1, keepdims=True))
        ).astype(BF16)
        gbase_ref[0] = grad_base
        gf_ref[0] = dot_t(grad_base, wskip_ref[:width]).astype(BF16)
        gs_ref[0] = dot_t(grad_base, wskip_ref[width:]).astype(BF16)

    @pl.when(jnp.logical_not(live))
    def _():
        for ref in (gbase_ref, gf_ref, gs_ref):
            ref[...] = jnp.zeros_like(ref)


def back_call(lengths, grad_proj, wqkv, base, grad_middle, gain, w_skip):
    units, length, width = base.shape
    groups, group_width = wqkv.shape[1], wqkv.shape[4]
    total = groups * group_width
    rows = row_block(length, 384)
    block = pl.BlockSpec((1, rows, width), lambda u, i, *_: (u, i, 0))
    unit = pl.BlockSpec((1, 1, width), lambda u, i, *_: (u, 0, 0))
    return call(
        functools.partial(back_kernel, rows=rows, width=width, groups=groups, group_width=group_width),
        (units, length // rows),
        [
            pl.BlockSpec((3, 1, rows, total), lambda u, i, *_: (0, u, i, 0)),
            whole(wqkv.shape),
            block,
            block,
            unit,
            whole(w_skip.shape),
        ],
        [block, block, block, unit],
        [
            jax.ShapeDtypeStruct(base.shape, BF16),
            jax.ShapeDtypeStruct(base.shape, BF16),
            jax.ShapeDtypeStruct(base.shape, BF16),
            jax.ShapeDtypeStruct((units, 1, width), F32),
        ],
        flops=units * length * width * (6 * total + 4 * width),
        nbytes=units * length * width * 20,
    )(lengths, grad_proj, wqkv, base, grad_middle, gain, w_skip)


def weight_grad(left, right):
    return lax.dot_general(left, right, (((0, 1), (0, 1)), ((), ())), preferred_element_type=F32)


def core(own, lengths, frames, skip, cotangent, gain_attn, gain_ffn, wqkv, wout, wup, wdown, bias, w_skip):
    cosine, sine = rope_tables(frames.shape[1])
    base, attn_in = base_call(lengths, frames, skip, w_skip, gain_attn)
    qkv = qkv_call(lengths, attn_in, wqkv, cosine, sine)
    context, stats = attn_call(lengths, qkv)
    mixed, ffn_in, act, grad_pre, grad_middle, grad_attn, grad_context, ggain_ffn, gbias = mid_call(
        lengths, own, context, base, cotangent, gain_ffn, wout, wup, wdown, bias
    )
    grad_proj = attn_back_call(lengths, qkv, context, grad_context, stats, cosine, sine)
    grad_base, grad_frames, grad_skip, ggain_attn = back_call(
        lengths, grad_proj, wqkv, base, grad_middle, gain_attn, w_skip
    )
    return dict(
        attn_in=attn_in,
        context=context,
        mixed=mixed,
        ffn_in=ffn_in,
        act=act,
        grad_pre=grad_pre,
        grad_attn=grad_attn,
        ggain_ffn=ggain_ffn,
        gbias=gbias,
        grad_proj=grad_proj,
        grad_base=grad_base,
        grad_frames=grad_frames,
        grad_skip=grad_skip,
        ggain_attn=ggain_attn,
    )


def gather_slices(weight, axis, ways, spot):
    size = weight.shape[axis] // ways
    piece = lax.dynamic_slice_in_dim(weight, spot * size, size, axis)
    every = lax.all_gather(piece, BOTH, axis=0)
    return every.reshape((ways, every.shape[0] // ways) + piece.shape)


def local(
    frames,
    skip_frames,
    cotangent,
    lengths,
    time_steps,
    time_table,
    w_skip,
    w_gamma_attn,
    w_gamma_ffn,
    w_qkv,
    w_out,
    w_up,
    b_up,
    w_down,
):
    micro_count, seq_count, length, width = frames.shape
    units = micro_count * seq_count
    ways = lax.axis_size("dp")
    shards = lax.axis_size("tensor")
    spot = lax.axis_index("dp")
    own = lax.axis_index("tensor")
    local_width = w_qkv.shape[2]
    hidden = w_up.shape[1]
    table_rows = time_table.shape[0]
    flat = (units, length, width)
    flat_lengths = lengths.reshape(units)
    flat_steps = time_steps.reshape(units)

    wqkv = gather_slices(w_qkv, 1, ways, spot)
    wout = gather_slices(w_out, 0, ways, spot)
    wup = gather_slices(w_up, 0, ways, spot)
    wdown = gather_slices(w_down, 0, ways, spot)
    bias = lax.all_gather(b_up, "tensor", axis=0).reshape(shards, 1, hidden)
    if local_width % LANES:
        merge = LANES * 2 // local_width
        wqkv = wqkv.reshape(ways, shards // merge, merge, 3, width // ways, local_width)
        wqkv = wqkv.transpose(1, 3, 0, 4, 2, 5).reshape(1, shards // merge, 3, width, LANES * 2)
        wout = wout.transpose(1, 0, 2, 3).reshape(1, shards // merge, LANES * 2, width)

    onehot = (flat_steps[:, None] == jnp.arange(table_rows)[None, :]).astype(BF16)
    condition = jnp.dot(onehot, time_table, preferred_element_type=F32).astype(BF16)
    gain_attn = 1.0 + jnp.dot(condition, w_gamma_attn, preferred_element_type=F32)
    gain_ffn = 1.0 + jnp.dot(condition, w_gamma_ffn, preferred_element_type=F32)

    r = core(
        own.reshape(1).astype(jnp.int32),
        flat_lengths,
        frames.reshape(flat),
        skip_frames.reshape(flat),
        cotangent.reshape(flat),
        gain_attn[:, None, :],
        gain_ffn[:, None, :],
        wqkv,
        wout,
        wup,
        wdown,
        bias,
        w_skip,
    )

    def own_heads(x):
        return lax.dynamic_slice_in_dim(x, own * local_width, local_width, x.ndim - 1)

    def scatter(grad, axis):
        return lax.psum_scatter(
            grad.astype(BF16), "dp", scatter_dimension=axis, tiled=True
        ).astype(F32)

    flat_cot = cotangent.reshape(flat)
    grad_w_down = scatter(weight_grad(r["act"], flat_cot), 1)
    grad_w_up = scatter(weight_grad(r["ffn_in"], r["grad_pre"]), 0)
    grad_w_out = scatter(weight_grad(own_heads(r["context"]), r["grad_attn"]), 1)
    own_proj = own_heads(r["grad_proj"])
    grad_w_qkv = scatter(jnp.stack([weight_grad(r["attn_in"], own_proj[c]) for c in range(3)]), 1)
    joined = jnp.concatenate([frames.reshape(flat), skip_frames.reshape(flat)], axis=-1)
    skip_rows = weight_grad(joined, r["grad_base"]).astype(BF16)
    part = skip_rows.shape[0] // (ways * shards)
    skip_rows = lax.dynamic_index_in_dim(
        skip_rows.reshape(ways, shards, part, width), own, 1, keepdims=False
    ).reshape(ways * part, width)
    grad_w_skip = scatter(skip_rows, 0)

    small = jnp.concatenate(
        [
            condition.astype(F32),
            r["ggain_attn"].reshape(units, width).astype(BF16).astype(F32),
            r["ggain_ffn"].reshape(units, width).astype(BF16).astype(F32),
            jnp.broadcast_to(flat_steps.astype(F32)[:, None], (units, width)),
            jnp.pad(jnp.sum(r["gbias"], axis=0), ((0, 0), (0, width - hidden))),
        ],
        axis=0,
    )
    every = lax.all_gather(small, "dp", axis=0)
    count = ways * units
    all_condition = every[:, :units].reshape(count, width).astype(BF16)
    all_attn = every[:, units : 2 * units].reshape(count, width).astype(BF16)
    all_ffn = every[:, 2 * units : 3 * units].reshape(count, width).astype(BF16)
    all_steps = every[:, 3 * units : 4 * units, 0].reshape(count)
    bias_grad = jnp.sum(every[:, 4 * units, :hidden], axis=0)
    rows = width // ways
    own_condition = lax.dynamic_slice_in_dim(all_condition, spot * rows, rows, 1)
    grad_gamma_attn = lax.dot_general(
        own_condition, all_attn, (((0,), (0,)), ((), ())), preferred_element_type=F32
    )
    grad_gamma_ffn = lax.dot_general(
        own_condition, all_ffn, (((0,), (0,)), ((), ())), preferred_element_type=F32
    )
    grad_condition = lax.dot_general(
        all_attn, w_gamma_attn, (((1,), (1,)), ((), ())), preferred_element_type=F32
    ) + lax.dot_general(all_ffn, w_gamma_ffn, (((1,), (1,)), ((), ())), preferred_element_type=F32)
    steps_here = table_rows // ways
    wanted = (spot * steps_here + jnp.arange(steps_here)).astype(F32)
    chosen = (wanted[:, None] == all_steps[None, :]).astype(F32)
    grad_table = jnp.dot(chosen, grad_condition, precision=lax.Precision.HIGHEST)

    back_shape = (micro_count, seq_count, length, width)
    return (
        r["mixed"].reshape(back_shape),
        r["grad_frames"].reshape(back_shape),
        r["grad_skip"].reshape(back_shape),
        grad_table,
        grad_w_skip,
        grad_gamma_attn,
        grad_gamma_ffn,
        grad_w_qkv,
        grad_w_out,
        grad_w_up,
        bias_grad,
        grad_w_down,
    )


def solution(mesh):
    placed = (
        P(None, "dp", None, None),
        P(None, "dp", None, None),
        P(None, "dp", None, None),
        P(None, "dp"),
        P(None, "dp"),
        P(),
        P(),
        P(),
        P(),
        P(None, None, "tensor"),
        P("tensor", None),
        P(None, "tensor"),
        P("tensor"),
        P("tensor", None),
    )
    return jax.shard_map(
        local,
        mesh=mesh,
        in_specs=placed,
        out_specs=(
            P(None, "dp", None, None),
            P(None, "dp", None, None),
            P(None, "dp", None, None),
            P("dp", None),
            P(("dp", "tensor"), None),
            P("dp", None),
            P("dp", None),
            P(None, "dp", "tensor"),
            P("tensor", "dp"),
            P("dp", "tensor"),
            P("tensor"),
            P("tensor", "dp"),
        ),
        check_vma=False,
    )
```

```python
import functools
import math

import jax
import jax.numpy as jnp
from jax import lax
from jax.experimental import pallas as pl
from jax.experimental.pallas import tpu as pltpu
from jax.sharding import PartitionSpec as P

HD = 64
LANES = 128
EPSILON = 1e-06
MASKED = -1e30
BF16 = jnp.bfloat16
F32 = jnp.float32
SCALE = 1.0 / math.sqrt(HD)
VMEM_BYTES = 62 * 1024 * 1024
BOTH = ("dp", "tensor")


def dot(a, b):
    return lax.dot_general(a, b, (((1,), (0,)), ((), ())), preferred_element_type=F32)


def dot_t(a, b):
    return lax.dot_general(a, b, (((1,), (1,)), ((), ())), preferred_element_type=F32)


def t_dot(a, b):
    return lax.dot_general(a, b, (((0,), (0,)), ((), ())), preferred_element_type=F32)


def rope_tables(length):
    lane = jnp.arange(LANES)
    half = HD // 2
    frequency = jnp.exp((lane % half).astype(F32) * (-2.0 * math.log(10000.0) / HD))
    angles = jnp.arange(length, dtype=F32)[:, None] * frequency[None, :]
    sign = jnp.where(lane % HD < half, -1.0, 1.0)
    return jnp.cos(angles), jnp.sin(angles) * sign[None, :]


def partner(x):
    lane = lax.broadcasted_iota(jnp.int32, x.shape, 1)
    return jnp.where(lane & (HD - 1) < HD // 2, pltpu.roll(x, LANES - HD // 2, 1), pltpu.roll(x, HD // 2, 1))


def head_masks(dtype):
    lane = lax.broadcasted_iota(jnp.int32, (1, LANES), 1)
    return (lane < HD).astype(dtype), (lane >= HD).astype(dtype)


def call(kernel, grid, in_specs, out_specs, out_shape, scratch=(), prefetch=1, flops=0, nbytes=0):
    return pl.pallas_call(
        kernel,
        out_shape=out_shape,
        grid_spec=pltpu.PrefetchScalarGridSpec(
            num_scalar_prefetch=prefetch,
            grid=grid,
            in_specs=in_specs,
            out_specs=out_specs,
            scratch_shapes=list(scratch),
        ),
        compiler_params=pltpu.CompilerParams(
            dimension_semantics=("arbitrary",) * len(grid), vmem_limit_bytes=VMEM_BYTES
        ),
        cost_estimate=pl.CostEstimate(flops=flops, bytes_accessed=nbytes, transcendentals=0),
    )


def whole(shape):
    return pl.BlockSpec(shape, lambda *_: (0,) * len(shape), pipeline_mode=pl.Buffered(1))


def row_block(length, wanted):
    for rows in (wanted, 384, 288, 192, 128, 64, 32, 16):
        if rows <= wanted and length % rows == 0:
            return rows
    return length


def base_kernel(len_ref, f_ref, s_ref, w_ref, g_ref, base_ref, ain_ref, *, rows, width):
    live = pl.program_id(1) * rows < len_ref[pl.program_id(0)]

    @pl.when(live)
    def _():
        acc = dot(f_ref[0], w_ref[:width]) + dot(s_ref[0], w_ref[width:])
        factor = lax.rsqrt(jnp.mean(acc * acc, axis=-1, keepdims=True) + EPSILON)
        base_ref[0] = acc
        ain_ref[0] = (acc * factor * g_ref[0]).astype(BF16)

    @pl.when(jnp.logical_not(live))
    def _():
        base_ref[...] = jnp.zeros_like(base_ref)
        ain_ref[...] = jnp.zeros_like(ain_ref)


def base_call(lengths, frames, skip, w_skip, gain):
    units, length, width = frames.shape
    rows = row_block(length, 384)
    block = pl.BlockSpec((1, rows, width), lambda u, i, *_: (u, i, 0))
    return call(
        functools.partial(base_kernel, rows=rows, width=width),
        (units, length // rows),
        [block, block, whole(w_skip.shape), pl.BlockSpec((1, 1, width), lambda u, i, *_: (u, 0, 0))],
        [block, block],
        [
            jax.ShapeDtypeStruct(frames.shape, F32),
            jax.ShapeDtypeStruct(frames.shape, BF16),
        ],
        flops=4 * units * length * width * width,
        nbytes=units * length * width * 10,
    )(lengths, frames, skip, w_skip, gain)


def qkv_kernel(len_ref, a_ref, w_ref, cos_ref, sin_ref, o_ref, *, rows, groups, width, group_width):
    live = pl.program_id(1) * rows < len_ref[pl.program_id(0)]

    @pl.when(live)
    def _():
        a = a_ref[0]
        cosine = cos_ref[...]
        sine = sin_ref[...]
        for g in range(groups):
            for c in range(3):
                y = dot(a, w_ref[:, g, c].reshape(width, group_width))
                for j in range(group_width // LANES):
                    part = y[:, j * LANES : (j + 1) * LANES]
                    if c < 2:
                        part = part * cosine + partner(part) * sine
                    if c == 0:
                        part = part * SCALE
                    at = g * group_width + j * LANES
                    o_ref[c, 0, :, at : at + LANES] = part.astype(BF16)

    @pl.when(jnp.logical_not(live))
    def _():
        o_ref[...] = jnp.zeros_like(o_ref)


def qkv_call(lengths, attn_in, wqkv, cosine, sine):
    units, length, width = attn_in.shape
    groups, group_width = wqkv.shape[1], wqkv.shape[4]
    total = groups * group_width
    rows = row_block(length, 384)
    table = pl.BlockSpec((rows, LANES), lambda u, i, *_: (i, 0))
    return call(
        functools.partial(qkv_kernel, rows=rows, groups=groups, width=width, group_width=group_width),
        (units, length // rows),
        [pl.BlockSpec((1, rows, width), lambda u, i, *_: (u, i, 0)), whole(wqkv.shape), table, table],
        pl.BlockSpec((3, 1, rows, total), lambda u, i, *_: (0, u, i, 0)),
        jax.ShapeDtypeStruct((3, units, length, total), BF16),
        flops=6 * units * length * width * total,
        nbytes=units * length * width * 8,
    )(lengths, attn_in, wqkv, cosine, sine)


def extents_of(length):
    step = length // 3
    return [e for e in (step, step + step * 2 // 3, 2 * step + step // 3, length) if e % 128 == 0]


def by_extent(n, extents, run):
    low = 0
    for e in extents:
        pl.when(jnp.logical_and(n > low, n <= e))(functools.partial(run, e, low))
        low = e


def attn_kernel(len_ref, q_ref, k_ref, v_ref, ctx_ref, st_ref, *, length, block, extents):
    u = pl.program_id(0)
    p = pl.program_id(1)
    n = len_ref[u]
    lane = lax.broadcasted_iota(jnp.int32, (block, LANES), 1)
    masks = head_masks(BF16)

    @pl.when(p == 0)
    def _():
        st_ref[...] = jnp.zeros_like(st_ref)

    def run(extent, low):
        keys = k_ref[0, 0, :extent]
        values = v_ref[0, 0, :extent]
        place = lax.broadcasted_iota(jnp.int32, (1, extent), 1)
        bias = jnp.where(place < n, 0.0, MASKED)

        def body(i, carry):
            at = pl.ds(pl.multiple_of(i * block, block), block)
            q = q_ref[0, 0, at]
            stats = st_ref[0, at]
            outs = []
            for h in range(2):
                s = dot_t(q * masks[h], keys) + bias
                m = jnp.max(s, axis=-1, keepdims=True)
                e = jnp.exp(s - m)
                l = jnp.sum(e, axis=-1, keepdims=True)
                outs.append(dot(e.astype(BF16), values) * (1.0 / l))
                stats = jnp.where(lane == 2 * p + h, m + jnp.log(l), stats)
            ctx_ref[0, at] = jnp.where(lane < HD, outs[0], outs[1]).astype(BF16)
            st_ref[0, at] = stats
            return carry

        lax.fori_loop(0, pl.cdiv(n, block), body, 0)

    by_extent(n, extents, run)

    def clear(i, carry):
        at = pl.ds(pl.multiple_of(i * block, block), block)
        ctx_ref[0, at] = jnp.zeros((block, LANES), BF16)
        return carry

    lax.fori_loop(pl.cdiv(n, block), length // block, clear, 0)


def attn_call(lengths, qkv):
    _, units, length, total = qkv.shape
    block = row_block(length, 384)
    pairs = total // LANES

    def part(c):
        return pl.BlockSpec((1, 1, length, LANES), lambda u, p, *_: (c, u, 0, p))

    return call(
        functools.partial(attn_kernel, length=length, block=block, extents=extents_of(length)),
        (units, pairs),
        [part(0), part(1), part(2)],
        [
            pl.BlockSpec((1, length, LANES), lambda u, p, *_: (u, 0, p)),
            pl.BlockSpec((1, length, LANES), lambda u, p, *_: (u, 0, 0)),
        ],
        [
            jax.ShapeDtypeStruct((units, length, total), BF16),
            jax.ShapeDtypeStruct((units, length, LANES), F32),
        ],
        flops=16 * units * length * length * total,
        nbytes=units * length * total * 8,
    )(lengths, qkv, qkv, qkv)


def mid_kernel(
    len_ref,
    own_ref,
    ctx_ref,
    base_ref,
    cot_ref,
    gain_ref,
    *refs,
    rows,
    width,
    groups,
    group_width,
    hidden,
    chunk,
    shards,
    places,
):
    weights = refs[: 1 + max(spot for spot, _, _ in places)]
    (
    mixed_ref,
    fin_ref,
    act_ref,
    gpre_ref,
    gmid_ref,
    gattn_ref,
    gctx_ref,
    ggain_ref,
    gbias_ref,
    out_acc,
    gin_acc,
    fin_s,
    cot_s,
    ) = refs[len(weights) :]

    def piece(which, g, cols=slice(None)):
        spot, low, count = places[which]
        part = weights[spot][:, g, low : low + count, cols]
        return part.reshape(part.shape[0] * count, part.shape[2])

    def bias_row(g, cols):
        spot, low, _ = places[1]
        return weights[spot][0, g, low : low + 1, cols].astype(F32)

    u = pl.program_id(0)
    i = pl.program_id(1)
    n = len_ref[u]
    own = own_ref[0]
    live = i * rows < n

    @pl.when(i == 0)
    def _():
        ggain_ref[...] = jnp.zeros_like(ggain_ref)
        gbias_ref[...] = jnp.zeros_like(gbias_ref)

    @pl.when(live)
    def _():
        place = i * rows + lax.broadcasted_iota(jnp.int32, (rows, 1), 0)
        row_live = (place < n).astype(F32)
        attn = jnp.zeros((rows, width), F32)
        for g in range(groups):
            w = piece(3, g)
            share = dot(ctx_ref[0, :, g * group_width : (g + 1) * group_width], w)
            attn = attn + share.astype(BF16).astype(F32)
        middle = base_ref[0] + attn
        factor = lax.rsqrt(jnp.mean(middle * middle, axis=-1, keepdims=True) + EPSILON)
        gain = gain_ref[0]
        gmid_ref[0] = middle
        fin_s[...] = (middle * factor * gain).astype(BF16)
        fin_ref[0] = fin_s[...]
        cot_s[...] = (cot_ref[0].astype(F32) * row_live).astype(BF16)
        out_acc[...] = jnp.zeros_like(out_acc)
        gin_acc[...] = jnp.zeros_like(gin_acc)

        def step(g, carry):
            share = jnp.zeros((rows, width), F32)
            back = jnp.zeros((rows, width), F32)
            for c in range(hidden // chunk):
                cols = slice(c * chunk, (c + 1) * chunk)
                up = piece(0, g, cols)
                down = piece(2, g)[cols]
                pre = dot(fin_s[...], up) + bias_row(g, cols)
                grad_act = dot_t(cot_s[...], down)
                phi = 0.5 + 0.5 * lax.erf(pre * math.sqrt(0.5))
                density = jnp.exp(-0.5 * pre * pre) * (1.0 / math.sqrt(2.0 * math.pi))
                act = (pre * phi).astype(BF16)
                grad_pre_wide = (phi + pre * density) * grad_act
                grad_pre = grad_pre_wide.astype(BF16)
                share = share + dot(act, down)
                back = back + dot_t(grad_pre, up)

                @pl.when(g == own)
                def _():
                    act_ref[0, :, cols] = (act.astype(F32) * row_live).astype(BF16)
                    gpre_ref[0, :, cols] = grad_pre
                    gbias_ref[0, :, cols] += jnp.sum(grad_pre.astype(F32), axis=0, keepdims=True)

            out_acc[...] += share.astype(BF16).astype(F32)
            gin_acc[...] += back.astype(BF16).astype(F32)
            return carry

        lax.fori_loop(0, shards, step, 0)
        middle = gmid_ref[0]
        factor = lax.rsqrt(jnp.mean(middle * middle, axis=-1, keepdims=True) + EPSILON)
        normed = middle * factor
        mixed_ref[0] = ((middle + out_acc[...]) * row_live).astype(BF16)
        grad_in = gin_acc[...]
        ggain_ref[0] += jnp.sum(grad_in * normed, axis=0, keepdims=True)
        dn = grad_in * gain
        grad_middle = cot_s[...].astype(F32) + factor * (
            dn - normed * jnp.mean(dn * normed, axis=-1, keepdims=True)
        )
        gmid_ref[0] = grad_middle
        grad_attn = grad_middle.astype(BF16)
        gattn_ref[0] = grad_attn
        for g in range(groups):
            w = piece(3, g)
            gctx_ref[0, :, g * group_width : (g + 1) * group_width] = dot_t(grad_attn, w).astype(BF16)

    @pl.when(jnp.logical_not(live))
    def _():
        for ref in (mixed_ref, fin_ref, act_ref, gpre_ref, gmid_ref, gattn_ref, gctx_ref):
            ref[...] = jnp.zeros_like(ref)


def mid_call(lengths, own, context, base, cotangent, gain, weights, places, groups, hidden, shards):
    units, length, width = base.shape
    total = context.shape[2]
    rows = row_block(length, 384)
    chunk = min(hidden, 512)

    def block(size):
        return pl.BlockSpec((1, rows, size), lambda u, i, *_: (u, i, 0))

    def unit(size):
        return pl.BlockSpec((1, 1, size), lambda u, i, *_: (u, 0, 0))

    def full(size, dtype):
        return jax.ShapeDtypeStruct((units, length, size), dtype)

    ff = shards * hidden
    return call(
        functools.partial(
            mid_kernel,
            rows=rows,
            width=width,
            groups=groups,
            group_width=total // groups,
            hidden=hidden,
            chunk=chunk,
            shards=shards,
            places=places,
        ),
        (units, length // rows),
        [
            block(total),
            block(width),
            block(width),
            unit(width),
            *[whole(w.shape) for w in weights],
        ],
        [
            block(width),
            block(width),
            block(hidden),
            block(hidden),
            block(width),
            block(width),
            block(total),
            unit(width),
            unit(hidden),
        ],
        [
            full(width, BF16),
            full(width, BF16),
            full(hidden, BF16),
            full(hidden, BF16),
            full(width, F32),
            full(width, BF16),
            full(total, BF16),
            jax.ShapeDtypeStruct((units, 1, width), F32),
            jax.ShapeDtypeStruct((units, 1, hidden), F32),
        ],
        scratch=[
            pltpu.VMEM((rows, width), F32),
            pltpu.VMEM((rows, width), F32),
            pltpu.VMEM((rows, width), BF16),
            pltpu.VMEM((rows, width), BF16),
        ],
        prefetch=2,
        flops=units * length * width * (8 * ff + 4 * total),
        nbytes=units * length * width * 26,
    )(lengths, own, context, base, cotangent, gain, *weights)


def attn_back_kernel(
    len_ref,
    q_ref,
    k_ref,
    v_ref,
    ctx_ref,
    gctx_ref,
    st_ref,
    cos_ref,
    sin_ref,
    o_ref,
    dq_s,
    stat_s,
    delta_s,
    *,
    length,
    block,
    extents,
):
    u = pl.program_id(0)
    p = pl.program_id(1)
    n = len_ref[u]
    masks = head_masks(BF16)

    @pl.when(p == 0)
    def _():
        stat_s[...] = st_ref[0].T

    product = ctx_ref[0].astype(F32) * gctx_ref[0].astype(F32)
    turned = product.T
    delta_s[0:1] = jnp.sum(turned[:HD], axis=0, keepdims=True)
    delta_s[1:2] = jnp.sum(turned[HD:], axis=0, keepdims=True)

    def unturn(x, at):
        return x * cos_ref[at] - partner(x) * sin_ref[at]

    def run(extent, low):
        q = q_ref[0, 0, :extent]
        gctx = gctx_ref[0, :extent]
        dq_s[...] = jnp.zeros_like(dq_s)
        lse = [stat_s[pl.ds(2 * p + h, 1), :extent] for h in range(2)]
        delta = [delta_s[h : h + 1, :extent] for h in range(2)]
        lane = lax.broadcasted_iota(jnp.int32, (block, LANES), 1)

        def body(i, carry):
            at = pl.ds(pl.multiple_of(i * block, block), block)
            keys = k_ref[0, 0, at]
            values = v_ref[0, 0, at]
            key_live = (i * block + lax.broadcasted_iota(jnp.int32, (block, 1), 0) < n)
            bias = jnp.where(key_live, 0.0, MASKED)
            grad_v, grad_k, grad_s, masked = [], [], [], []
            for h in range(2):
                kh = keys * masks[h]
                s = dot_t(kh, q)
                probs = jnp.exp(s + bias - lse[h])
                grad_v.append(dot(probs.astype(BF16), gctx))
                gp = dot_t(values * masks[h], gctx)
                gs = (probs * (gp - delta[h])).astype(BF16)
                grad_k.append(dot(gs, q))
                grad_s.append(gs)
                masked.append(kh)
            dq_s[:extent] += t_dot(jnp.concatenate(grad_s, axis=0), jnp.concatenate(masked, axis=0))
            gk = jnp.where(lane < HD, grad_k[0], grad_k[1])
            gv = jnp.where(lane < HD, grad_v[0], grad_v[1])
            o_ref[1, 0, at] = unturn(gk, at).astype(BF16)
            o_ref[2, 0, at] = gv.astype(BF16)
            return carry

        lax.fori_loop(0, pl.cdiv(n, block), body, 0)

    by_extent(n, extents, run)

    def finish(i, carry):
        at = pl.ds(pl.multiple_of(i * block, block), block)
        o_ref[0, 0, at] = (unturn(dq_s[at], at) * SCALE).astype(BF16)
        return carry

    def clear(i, carry):
        at = pl.ds(pl.multiple_of(i * block, block), block)
        for c in range(3):
            o_ref[c, 0, at] = jnp.zeros((block, LANES), BF16)
        return carry

    lax.fori_loop(0, pl.cdiv(n, block), finish, 0)
    lax.fori_loop(pl.cdiv(n, block), length // block, clear, 0)


def attn_back_call(lengths, qkv, context, grad_context, stats, cosine, sine):
    _, units, length, total = qkv.shape
    block = row_block(length, 384)
    pairs = total // LANES

    def part(c):
        return pl.BlockSpec((1, 1, length, LANES), lambda u, p, *_: (c, u, 0, p))

    lanes = pl.BlockSpec((1, length, LANES), lambda u, p, *_: (u, 0, p))
    return call(
        functools.partial(attn_back_kernel, length=length, block=block, extents=extents_of(length)),
        (units, pairs),
        [
            part(0),
            part(1),
            part(2),
            lanes,
            lanes,
            pl.BlockSpec((1, length, LANES), lambda u, p, *_: (u, 0, 0)),
            whole((length, LANES)),
            whole((length, LANES)),
        ],
        pl.BlockSpec((3, 1, length, LANES), lambda u, p, *_: (0, u, 0, p)),
        jax.ShapeDtypeStruct((3, units, length, total), BF16),
        scratch=[
            pltpu.VMEM((length, LANES), F32),
            pltpu.VMEM((LANES, length), F32),
            pltpu.VMEM((8, length), F32),
        ],
        flops=40 * units * length * length * total,
        nbytes=units * length * total * 16,
    )(lengths, qkv, qkv, qkv, context, grad_context, stats, cosine, sine)


def back_kernel(
    len_ref,
    gp_ref,
    w_ref,
    base_ref,
    gmid_ref,
    gain_ref,
    wskip_ref,
    gbase_ref,
    gf_ref,
    gs_ref,
    ggain_ref,
    *,
    rows,
    width,
    groups,
    group_width,
):
    u = pl.program_id(0)
    i = pl.program_id(1)
    live = i * rows < len_ref[u]

    @pl.when(i == 0)
    def _():
        ggain_ref[...] = jnp.zeros_like(ggain_ref)

    @pl.when(live)
    def _():
        grad_in = jnp.zeros((rows, width), F32)
        for g in range(groups):
            cols = slice(g * group_width, (g + 1) * group_width)
            share = jnp.zeros((rows, width), F32)
            for c in range(3):
                share = share + dot_t(gp_ref[c, 0, :, cols], w_ref[:, g, c].reshape(width, group_width))
            grad_in = grad_in + share.astype(BF16).astype(F32)
        base = base_ref[0]
        factor = lax.rsqrt(jnp.mean(base * base, axis=-1, keepdims=True) + EPSILON)
        normed = base * factor
        ggain_ref[0] += jnp.sum(grad_in * normed, axis=0, keepdims=True)
        dm = grad_in * gain_ref[0]
        grad_base = (
            gmid_ref[0] + factor * (dm - normed * jnp.mean(dm * normed, axis=-1, keepdims=True))
        ).astype(BF16)
        gbase_ref[0] = grad_base
        gf_ref[0] = dot_t(grad_base, wskip_ref[:width]).astype(BF16)
        gs_ref[0] = dot_t(grad_base, wskip_ref[width:]).astype(BF16)

    @pl.when(jnp.logical_not(live))
    def _():
        for ref in (gbase_ref, gf_ref, gs_ref):
            ref[...] = jnp.zeros_like(ref)


def back_call(lengths, grad_proj, wqkv, base, grad_middle, gain, w_skip):
    units, length, width = base.shape
    groups, group_width = wqkv.shape[1], wqkv.shape[4]
    total = groups * group_width
    rows = row_block(length, 384)
    block = pl.BlockSpec((1, rows, width), lambda u, i, *_: (u, i, 0))
    unit = pl.BlockSpec((1, 1, width), lambda u, i, *_: (u, 0, 0))
    return call(
        functools.partial(back_kernel, rows=rows, width=width, groups=groups, group_width=group_width),
        (units, length // rows),
        [
            pl.BlockSpec((3, 1, rows, total), lambda u, i, *_: (0, u, i, 0)),
            whole(wqkv.shape),
            block,
            block,
            unit,
            whole(w_skip.shape),
        ],
        [block, block, block, unit],
        [
            jax.ShapeDtypeStruct(base.shape, BF16),
            jax.ShapeDtypeStruct(base.shape, BF16),
            jax.ShapeDtypeStruct(base.shape, BF16),
            jax.ShapeDtypeStruct((units, 1, width), F32),
        ],
        flops=units * length * width * (6 * total + 4 * width),
        nbytes=units * length * width * 20,
    )(lengths, grad_proj, wqkv, base, grad_middle, gain, w_skip)


def product_kernel(len_ref, own_ref, *refs, rows, parts):
    u = pl.program_id(0)
    i = pl.program_id(1)
    o_ref, acc = refs[-2:]
    first = jnp.logical_and(u == 0, i == 0)
    last = jnp.logical_and(u == pl.num_programs(0) - 1, i == pl.num_programs(1) - 1)

    @pl.when(first)
    def _():
        acc[...] = jnp.zeros_like(acc)

    @pl.when(i * rows < len_ref[u])
    def _():
        low = 0
        for left, right, size in parts:
            a = refs[left][0]
            b = refs[right][...].reshape(rows, size)
            acc[:, low : low + size] += t_dot(a, b)
            low += size

    @pl.when(last)
    def _():
        o_ref[...] = acc[...].astype(BF16)


def product_call(lengths, own, lefts, rights):
    units, length, width = lefts[0].shape
    rows = row_block(length, 384)
    specs = [pl.BlockSpec((1, rows, width), lambda u, i, *_: (u, i, 0)) for _ in lefts]
    operands, parts = list(lefts), []
    for left, array, size, plane, cut in rights:

        def spot(u, i, lengths, own, plane=plane, cut=cut):
            at = (u, i, own[0] if cut else 0)
            return at if plane is None else (plane,) + at

        parts.append((left, len(operands), size))
        operands.append(array)
        specs.append(pl.BlockSpec((1,) * (array.ndim - 2) + (rows, size), spot))
    total = sum(size for _, _, size in parts)
    return call(
        functools.partial(product_kernel, rows=rows, parts=parts),
        (units, length // rows),
        specs,
        pl.BlockSpec((width, total), lambda *_: (0, 0), pipeline_mode=pl.Buffered(1)),
        jax.ShapeDtypeStruct((width, total), BF16),
        scratch=[pltpu.VMEM((width, total), F32)],
        prefetch=2,
        flops=2 * units * length * width * total,
        nbytes=2 * units * length * (len(lefts) * width + total),
    )(lengths, own, *operands)


def weight_grad(left, right):
    return lax.dot_general(left, right, (((0, 1), (0, 1)), ((), ())), preferred_element_type=F32)


def core(own, local_width, lengths, frames, skip, cotangent, gain_attn, gain_ffn, wqkv, mid_weights, places, hidden, shards, w_skip):
    cosine, sine = rope_tables(frames.shape[1])

    whole_lanes = local_width % LANES == 0

    def own_heads(x):
        if whole_lanes:
            return x
        return lax.dynamic_slice_in_dim(x, own[0] * local_width, local_width, x.ndim - 1)

    base, attn_in = base_call(lengths, frames, skip, w_skip, gain_attn)
    qkv = qkv_call(lengths, attn_in, wqkv, cosine, sine)
    context, stats = attn_call(lengths, qkv)
    mixed, ffn_in, act, grad_pre, grad_middle, grad_attn, grad_context, ggain_ffn, gbias = mid_call(
        lengths, own, context, base, cotangent, gain_ffn, mid_weights, places, wqkv.shape[1], hidden, shards
    )
    mid_grads = product_call(
        lengths,
        own,
        [ffn_in, cotangent, grad_attn],
        [
            (0, grad_pre, hidden, None, False),
            (1, act, hidden, None, False),
            (2, own_heads(context), local_width, None, whole_lanes),
        ],
    )
    mid_grads, grad_context = lax.optimization_barrier((mid_grads, grad_context))
    grad_proj = attn_back_call(lengths, qkv, context, grad_context, stats, cosine, sine)
    own_proj = own_heads(grad_proj)
    proj = product_call(
        lengths, own, [attn_in], [(0, own_proj, local_width, c, whole_lanes) for c in range(3)]
    )
    proj, grad_proj = lax.optimization_barrier((proj, grad_proj))
    grad_base, grad_frames, grad_skip, ggain_attn = back_call(
        lengths, grad_proj, wqkv, base, grad_middle, gain_attn, w_skip
    )
    joined = jnp.concatenate([frames, skip], axis=-1)
    skip_rows = weight_grad(joined, grad_base).astype(BF16)
    return dict(
        mixed=mixed,
        grad_frames=grad_frames,
        grad_skip=grad_skip,
        ggain_ffn=ggain_ffn,
        ggain_attn=ggain_attn,
        gbias=gbias,
        mid_grads=mid_grads,
        proj=proj,
        skip_rows=skip_rows,
    )


def swap(x, bit):
    return lax.ppermute(x, "dp", [(i, i ^ (1 << bit)) for i in range(lax.axis_size("dp"))])


def halving_scatter(x, spot, ways):
    bits = ways.bit_length() - 1
    acc = x.reshape((2,) * bits + x.shape[1:])
    for bit in range(bits):
        axis = bits - 1 - bit
        side = (spot >> bit) & 1
        keep = lax.dynamic_index_in_dim(acc, side, axis, keepdims=True)
        give = lax.dynamic_index_in_dim(acc, 1 - side, axis, keepdims=True)
        acc = keep.astype(F32) + swap(give.astype(BF16), bit).astype(F32)
    return acc.reshape(x.shape[1:])


def doubling_gather(x, ways):
    for bit in range(ways.bit_length() - 1):
        x = jnp.concatenate([x, swap(x, bit)], axis=0)
    return x


def gather_pieces(piece, ways):
    every = lax.all_gather(piece, BOTH, axis=0)
    return every.reshape((ways, every.shape[0] // ways) + piece.shape)


def gather_slices(weight, axis, ways, spot):
    size = weight.shape[axis] // ways
    return gather_pieces(lax.dynamic_slice_in_dim(weight, spot * size, size, axis), ways)


def local(
    frames,
    skip_frames,
    cotangent,
    lengths,
    time_steps,
    time_table,
    w_skip,
    w_gamma_attn,
    w_gamma_ffn,
    w_qkv,
    w_out,
    w_up,
    b_up,
    w_down,
):
    micro_count, seq_count, length, width = frames.shape
    units = micro_count * seq_count
    ways = lax.axis_size("dp")
    shards = lax.axis_size("tensor")
    spot = lax.axis_index("dp")
    own = lax.axis_index("tensor")
    local_width = w_qkv.shape[2]
    hidden = w_up.shape[1]
    table_rows = time_table.shape[0]
    flat = (units, length, width)
    flat_lengths = lengths.reshape(units)
    flat_steps = time_steps.reshape(units)

    wqkv = gather_slices(w_qkv, 1, ways, spot)
    bias = jnp.pad(b_up[None, :], ((0, 15), (0, 0)))
    up_rows, down_rows, out_rows = width // ways, hidden // ways, local_width // ways

    def slice_of(weight, size):
        return lax.dynamic_slice_in_dim(weight, spot * size, size, 0)

    up_piece = jnp.concatenate([slice_of(w_up, up_rows), bias], axis=0)
    down_piece = slice_of(w_down, down_rows)
    out_piece = slice_of(w_out, out_rows)
    if hidden == width and out_rows % 16 == 0:
        packed = gather_pieces(jnp.concatenate([up_piece, down_piece, out_piece], axis=0), ways)
        mid_weights = (packed,)
        at = up_rows + 16
        places = (
            (0, 0, up_rows),
            (0, up_rows, 1),
            (0, at, down_rows),
            (0, at + down_rows, out_rows),
        )
    else:
        wout = gather_pieces(out_piece, ways)
        merge = max(1, LANES * 2 // local_width)
        wout = wout.transpose(1, 0, 2, 3).reshape(1, shards // merge, merge * local_width, width)
        mid_weights = (gather_pieces(up_piece, ways), gather_pieces(down_piece, ways), wout)
        places = ((0, 0, up_rows), (0, up_rows, 1), (1, 0, down_rows), (2, 0, merge * local_width))
    if local_width % LANES:
        merge = LANES * 2 // local_width
        wqkv = wqkv.reshape(ways, shards // merge, merge, 3, width // ways, local_width)
        wqkv = wqkv.transpose(1, 3, 0, 4, 2, 5).reshape(1, shards // merge, 3, width, LANES * 2)

    onehot = (flat_steps[:, None] == jnp.arange(table_rows)[None, :]).astype(BF16)
    condition = jnp.dot(onehot, time_table, preferred_element_type=F32).astype(BF16)
    gain_attn = 1.0 + jnp.dot(condition, w_gamma_attn, preferred_element_type=F32)
    gain_ffn = 1.0 + jnp.dot(condition, w_gamma_ffn, preferred_element_type=F32)

    r = core(
        own.reshape(1).astype(jnp.int32),
        local_width,
        flat_lengths,
        frames.reshape(flat),
        skip_frames.reshape(flat),
        cotangent.reshape(flat),
        gain_attn[:, None, :],
        gain_ffn[:, None, :],
        wqkv,
        mid_weights,
        places,
        hidden,
        shards,
        w_skip,
    )

    def scatter(grad):
        return lax.psum_scatter(grad, "dp", scatter_dimension=0, tiled=True).astype(F32)

    mid_grads = scatter(r["mid_grads"])
    grad_w_up = mid_grads[:, :hidden]
    grad_w_down = mid_grads[:, hidden : 2 * hidden].T
    grad_w_out = mid_grads[:, 2 * hidden :].T
    grad_w_qkv = scatter(r["proj"]).reshape(width // ways, 3, local_width).transpose(1, 0, 2)
    skip_rows = r["skip_rows"]
    part = skip_rows.shape[0] // (ways * shards)
    skip_rows = lax.dynamic_index_in_dim(
        skip_rows.reshape(ways, shards, part, width), own, 1, keepdims=False
    )
    grad_w_skip = halving_scatter(skip_rows, spot, ways)

    small = jnp.concatenate(
        [
            condition.astype(F32),
            r["ggain_attn"].reshape(units, width).astype(BF16).astype(F32),
            r["ggain_ffn"].reshape(units, width).astype(BF16).astype(F32),
            jnp.broadcast_to(flat_steps.astype(F32)[:, None], (units, width)),
            jnp.pad(jnp.sum(r["gbias"], axis=0), ((0, 0), (0, width - hidden))),
        ],
        axis=0,
    )
    every = doubling_gather(small[None], ways)
    count = ways * units
    all_condition = every[:, :units].reshape(count, width).astype(BF16)
    all_attn = every[:, units : 2 * units].reshape(count, width).astype(BF16)
    all_ffn = every[:, 2 * units : 3 * units].reshape(count, width).astype(BF16)
    all_steps = every[:, 3 * units : 4 * units, 0].reshape(count)
    bias_grad = jnp.sum(every[:, 4 * units, :hidden], axis=0)
    rows = width // ways
    own_condition = lax.dynamic_slice_in_dim(all_condition, spot * rows, rows, 1)
    grad_gamma_attn = lax.dot_general(
        own_condition, all_attn, (((0,), (0,)), ((), ())), preferred_element_type=F32
    )
    grad_gamma_ffn = lax.dot_general(
        own_condition, all_ffn, (((0,), (0,)), ((), ())), preferred_element_type=F32
    )
    grad_condition = lax.dot_general(
        all_attn, w_gamma_attn, (((1,), (1,)), ((), ())), preferred_element_type=F32
    ) + lax.dot_general(all_ffn, w_gamma_ffn, (((1,), (1,)), ((), ())), preferred_element_type=F32)
    steps_here = table_rows // ways
    wanted = (spot * steps_here + jnp.arange(steps_here)).astype(F32)
    chosen = (wanted[:, None] == all_steps[None, :]).astype(F32)
    grad_table = jnp.dot(chosen, grad_condition, precision=lax.Precision.HIGHEST)

    back_shape = (micro_count, seq_count, length, width)
    return (
        r["mixed"].reshape(back_shape),
        r["grad_frames"].reshape(back_shape),
        r["grad_skip"].reshape(back_shape),
        grad_table,
        grad_w_skip,
        grad_gamma_attn,
        grad_gamma_ffn,
        grad_w_qkv,
        grad_w_out,
        grad_w_up,
        bias_grad,
        grad_w_down,
    )


def solution(mesh):
    placed = (
        P(None, "dp", None, None),
        P(None, "dp", None, None),
        P(None, "dp", None, None),
        P(None, "dp"),
        P(None, "dp"),
        P(),
        P(),
        P(),
        P(),
        P(None, None, "tensor"),
        P("tensor", None),
        P(None, "tensor"),
        P("tensor"),
        P("tensor", None),
    )
    return jax.shard_map(
        local,
        mesh=mesh,
        in_specs=placed,
        out_specs=(
            P(None, "dp", None, None),
            P(None, "dp", None, None),
            P(None, "dp", None, None),
            P("dp", None),
            P(("dp", "tensor"), None),
            P("dp", None),
            P("dp", None),
            P(None, "dp", "tensor"),
            P("tensor", "dp"),
            P("dp", "tensor"),
            P("tensor"),
            P("tensor", "dp"),
        ),
        check_vma=False,
    )
```
